32 devices in a mesh: groups: 2 (over y), ctx: 4 (over z), head: 4 (over x, core).
Axes of the slice: x: 2, y: 2, z: 4, core: 2. Of those that a mesh axis runs over, the one named last changes fastest.
Arguments:
- queries: bfloat16 [2, 512, 4096], P(None, ('groups', 'ctx'), 'head'), parts along dimension 1, may hold values from -8 to 8
- keys: bfloat16 [2, 512, 1024], P(None, ('groups', 'ctx'), 'head'), parts along dimension 1, may hold values from -8 to 8
- values: bfloat16 [2, 512, 1024], P(None, ('groups', 'ctx'), 'head'), parts along dimension 1, may hold values from -6 to 6
- residual: bfloat16 [2, 512, 4096], P(None, ('groups', 'ctx'), 'head'), parts along dimension 1, may hold values from -6 to 6
- targets: bfloat16 [2, 512, 4096], P(None, ('groups', 'ctx'), 'head'), parts along dimension 1, may hold values from -6 to 6
- lang_ids: int32 [2, 512], P(None, ('groups', 'ctx')), parts along dimension 1, may hold values from 0 to 15
- lang_scale: float32 [16, 4096], P(None, 'head'), may hold values from 0.25 to 2
- out_weight: bfloat16 [4096, 4096], P('head'), may hold values from -0.09375 to 0.09375
Outputs:
- grad_queries: float32 [2, 512, 4096], P(None, ('groups', 'ctx'), 'head'), parts along dimension 1
- grad_keys: float32 [2, 512, 1024], P(None, ('groups', 'ctx'), 'head'), parts along dimension 1
- grad_values: float32 [2, 512, 1024], P(None, ('groups', 'ctx'), 'head'), parts along dimension 1
The draws below stay inside these ranges and needn't reach their ends.
There are 2 independent parts, one for each index of `groups`. The reference program is written for one: setup_inputs(seed, part) draws one part's arguments, and reference() takes and returns one part's arrays. A program takes and returns all parts, laid end to end along the dimension named above; an argument that names none is the same for every part. Nothing has to cross between parts.
All inputs are finite; a program needn't handle non-finite values.
Results may differ from the reference program's by a relative error of at most 0.0062.
Values may be sent and summed in bfloat16 or wider, within the bound.
No kernel may reach another device: no remote copies, remote signals or barrier semaphores. Data moves between devices by JAX's collectives and lax.ppermute only.
A program may use at most 64 MiB of HBM per device.

```python
import jax
import jax.numpy as jnp
from jax import lax

D = 4096
HEADS = 32
KV_HEADS = 8
HEAD_DIM = 128
NLANG = 16
SPAN = 64
HALF = 256
SEQ = 512
N_CTX = 4


def base_law(key, shape):
    drawn = 1.4 * jax.random.normal(key, shape, jnp.float32)
    return jnp.clip(drawn, -8.0, 8.0)


def draw_queries(key, part):
    drawn = base_law(jax.random.fold_in(key, 11), (2, HALF, HEADS * HEAD_DIM))
    return drawn.astype(jnp.bfloat16)


def draw_keys(key, part):
    drawn = base_law(jax.random.fold_in(key, 13), (2, HALF, KV_HEADS * HEAD_DIM))
    return drawn.astype(jnp.bfloat16)


def with_ends(result, rng, least, largest):
    longest = result.shape.index(max(result.shape))
    spots = []
    for shift in (0, 1):
        where = [jax.random.randint(jax.random.fold_in(rng, axis), (), 0, length) for axis, length in enumerate(result.shape)]
        where[longest] = (where[longest] + shift) % result.shape[longest]
        spots.append(tuple(where))
    return result.at[spots[0]].set(least).at[spots[1]].set(largest)


def steps_of(rng, dims, cuts, low, largest):
    def one(dim, shards_of):
        draws = jax.random.uniform(jax.random.fold_in(jax.random.fold_in(rng, 6), dim), (shards_of,), jnp.float32, low / len(cuts), largest / len(cuts))
        return jnp.repeat(jnp.exp(draws), dims[dim] // shards_of).reshape((-1,) + (1,) * (len(dims) - dim - 1))

    level = one(*cuts[0])
    for cut in cuts[1:]:
        level = level * one(*cut)
    return level


def gaussian(rng, dims, deviation, limit, cuts=(), held_as=jnp.bfloat16):
    factor_of = steps_of(rng, dims, cuts, -0.22, 0.18) if cuts else 1.0
    array = jax.random.normal(rng, dims, jnp.float32) * deviation * factor_of
    return jnp.minimum(jnp.maximum(array, -limit), limit).astype(held_as)


def setup_inputs(seed: int = 0, part: int = 0) -> dict:
    arg_keys = jax.random.split(jax.random.key(seed), 9)
    own_keys = jax.random.split(jax.random.fold_in(arg_keys[8], part), 9)
    queries = draw_queries(jax.random.fold_in(jax.random.fold_in(arg_keys[8], part), 71), part)
    keys = draw_keys(jax.random.fold_in(jax.random.fold_in(arg_keys[8], part), 71), part)
    values = gaussian(own_keys[2], (2, HALF, KV_HEADS * HEAD_DIM), 1.0, 6.0, ((1, 4), (2, 4)))
    residual = gaussian(own_keys[3], (2, HALF, D), 1.0, 6.0, ((1, 4), (2, 4)))
    targets = gaussian(own_keys[4], (2, HALF, D), 1.0, 6.0, ((1, 4), (2, 4)))
    lang_ids = with_ends(jax.random.randint(own_keys[5], (2, HALF), 0, NLANG), jax.random.fold_in(own_keys[5], 1), 0, NLANG - 1).astype(jnp.int32)
    lang_scale = jnp.clip(0.25 + 1.75 * jax.random.uniform(arg_keys[6], (NLANG, D), jnp.float32) ** steps_of(arg_keys[6], (NLANG, D), ((1, 4),), -0.2, 0.2), 0.25, 2.0)
    out_weight = gaussian(arg_keys[7], (HEADS * HEAD_DIM, D), (HEADS * HEAD_DIM) ** -0.5, 0.09375, ((0, 4),))
    return dict(queries=queries, keys=keys, values=values, residual=residual, targets=targets, lang_ids=lang_ids, lang_scale=lang_scale, out_weight=out_weight)


def fold_positions():
    rows = jnp.arange(HALF, dtype=jnp.int32)
    blocks = rows // SPAN
    offsets = rows % SPAN
    upper = (2 * N_CTX - 1 - blocks) * SPAN + offsets
    return jnp.concatenate([rows, upper]).astype(jnp.int32)


def reference(queries, keys, values, residual, targets, lang_ids, lang_scale, out_weight):
    per_group = HEADS // KV_HEADS
    score_scale = HEAD_DIM ** -0.5
    positions = fold_positions()
    allowed = positions[None, :] <= positions[:, None]
    query_heads = queries.reshape(SEQ, HEADS, HEAD_DIM).transpose(1, 0, 2)
    key_heads = jnp.repeat(keys.reshape(SEQ, KV_HEADS, HEAD_DIM).transpose(1, 0, 2), per_group, axis=0)
    value_heads = jnp.repeat(values.reshape(SEQ, KV_HEADS, HEAD_DIM).transpose(1, 0, 2), per_group, axis=0)

    def forward_head(operands):
        query_rows, key_rows, value_rows = operands
        scores = jnp.dot(query_rows, key_rows.T, preferred_element_type=jnp.float32) * score_scale
        masked = jnp.where(allowed, scores, -jnp.inf)
        top = jnp.max(masked, axis=-1)
        log_norm = top + jnp.log(jnp.sum(jnp.exp(masked - top[:, None]), axis=-1))
        weights = jnp.exp(masked - log_norm[:, None])
        mixed = jnp.dot(weights, value_rows.astype(jnp.float32), precision=lax.Precision.HIGHEST).astype(jnp.bfloat16)
        return mixed, log_norm

    attended, log_norms = lax.map(forward_head, (query_heads, key_heads, value_heads))
    flat_attn = attended.transpose(1, 0, 2).reshape(SEQ, HEADS * HEAD_DIM)
    projected = jnp.dot(flat_attn, out_weight, preferred_element_type=jnp.float32)
    row_scales = lang_scale[lang_ids.reshape(SEQ)]
    hidden = residual.reshape(SEQ, D).astype(jnp.float32) + projected * row_scales
    wanted = targets.reshape(SEQ, D)[positions].astype(jnp.float32)
    grad_proj = ((hidden - wanted) * row_scales).astype(jnp.bfloat16)
    grad_attn = jnp.dot(grad_proj, out_weight.T, preferred_element_type=jnp.float32).astype(jnp.bfloat16)
    grad_out = grad_attn.reshape(SEQ, HEADS, HEAD_DIM).transpose(1, 0, 2)
    deltas = jnp.sum(grad_out.astype(jnp.float32) * attended.astype(jnp.float32), axis=-1)

    def backward_head(operands):
        query_rows, key_rows, value_rows, grad_rows, log_norm, delta = operands
        scores = jnp.dot(query_rows, key_rows.T, preferred_element_type=jnp.float32) * score_scale
        probs = jnp.exp(jnp.where(allowed, scores - log_norm[:, None], -jnp.inf))
        grad_value = jnp.dot(probs.astype(jnp.bfloat16).T, grad_rows, preferred_element_type=jnp.float32)
        grad_prob = jnp.dot(grad_rows, value_rows.T, preferred_element_type=jnp.float32)
        grad_scores = (probs * (grad_prob - delta[:, None])).astype(jnp.bfloat16)
        grad_query = jnp.dot(grad_scores, key_rows, preferred_element_type=jnp.float32) * score_scale
        grad_key = jnp.dot(grad_scores.T, query_rows, preferred_element_type=jnp.float32) * score_scale
        return grad_query, grad_key, grad_value

    grad_query, grad_key, grad_value = lax.map(backward_head, (query_heads, key_heads, value_heads, grad_out, log_norms, deltas))
    grad_key = grad_key.reshape(KV_HEADS, per_group, SEQ, HEAD_DIM).sum(axis=1)
    grad_value = grad_value.reshape(KV_HEADS, per_group, SEQ, HEAD_DIM).sum(axis=1)
    grad_queries = grad_query.transpose(1, 0, 2).reshape(2, HALF, HEADS * HEAD_DIM).astype(jnp.float32)
    grad_keys = grad_key.transpose(1, 0, 2).reshape(2, HALF, KV_HEADS * HEAD_DIM).astype(jnp.float32)
    grad_values = grad_value.transpose(1, 0, 2).reshape(2, HALF, KV_HEADS * HEAD_DIM).astype(jnp.float32)
    return (grad_queries, grad_keys, grad_values)
```

```python
import functools

import jax
import jax.numpy as jnp
from jax import lax
from jax.experimental import pallas as pl
from jax.experimental.pallas import tpu as pltpu
from jax.sharding import PartitionSpec as P

HEAD_DIM = 128
BIG_NEG = -1e30
LOG2E = 1.4426950408889634
F32 = jnp.float32
BF16 = jnp.bfloat16
VMEM = pl.BlockSpec(memory_space=pltpu.VMEM)
ANY = pl.BlockSpec(memory_space=pl.ANY)


def across(block, axis, bit):
    count = lax.axis_size(axis)
    return lax.ppermute(block, axis, [(i, i ^ bit) for i in range(count)])


def bits_of(count):
    return [1 << b for b in range(count.bit_length() - 1)]


def gather_blocks(own, axis):
    blocks = {0: own}
    for bit in reversed(bits_of(lax.axis_size(axis))):
        for s in sorted(blocks):
            blocks[s ^ bit] = across(blocks[s], axis, bit)
    return [blocks[s] for s in range(len(blocks))]


def nt(a, b):
    return lax.dot_general(a, b, (((1,), (1,)), ((), ())), preferred_element_type=F32)


def nn(a, b):
    return jnp.dot(a, b, preferred_element_type=F32)


def call(body, out, args, specs, mib, name, cost=None):
    return pl.pallas_call(
        body,
        out_shape=out,
        in_specs=specs,
        out_specs=jax.tree.map(lambda _: VMEM, out),
        compiler_params=pltpu.CompilerParams(vmem_limit_bytes=mib << 20),
        cost_estimate=cost,
        name=name,
    )(*args)


def cost(flops, moved):
    return pl.CostEstimate(flops=flops, bytes_accessed=moved, transcendentals=0)


def stacked_heads(ref, span, rows, group, per_group):
    pieces = [
        ref[span * rows : (span + 1) * rows, h * HEAD_DIM : (h + 1) * HEAD_DIM]
        for h in range(group * per_group, (group + 1) * per_group)
    ]
    return jnp.concatenate(pieces, axis=0)


def stacked_keys(refs, part, rows, group):
    cols = slice(group * HEAD_DIM, (group + 1) * HEAD_DIM)
    return jnp.concatenate([r[part * rows : (part + 1) * rows, cols] for r in refs], axis=0)


def diagonal_mask(owner_xor, device, rows, columns, upper):
    owner = device ^ owner_xor
    key = lax.broadcasted_iota(jnp.int32, (rows, columns), 0)
    query = lax.broadcasted_iota(jnp.int32, (rows, columns), 1) & (rows - 1)
    ahead = (device - owner if upper else owner - device) * rows
    return key + ahead <= query


def attention_kernel(n, rows, kv_local, per_group, q_ref, *refs):
    kv_refs, (att_ref, low_ref, high_ref) = refs[:n], refs[n:]
    device = lax.axis_index("ctx")
    columns = per_group * rows
    scale = HEAD_DIM**-0.5 * LOG2E
    masks = {
        (s, upper): diagonal_mask(s, device, rows, columns, upper)
        for s in range(n)
        for upper in (False, True)
    }
    for group in range(kv_local):
        keys = [stacked_keys(kv_refs, part, rows, group) for part in (0, 1)]
        vals = [stacked_keys(kv_refs, part, rows, group) for part in (2, 3)]
        vals_t = [v.astype(F32).T.astype(BF16) for v in vals]
        for span in (0, 1):
            query = stacked_heads(q_ref, span, rows, group, per_group)
            tiles = []
            for half in range(span + 1):
                tile = nt(keys[half], query) * scale
                if half == span:
                    tile = jnp.concatenate(
                        [
                            jnp.where(
                                masks[s, span == 1], tile[s * rows : (s + 1) * rows], BIG_NEG
                            )
                            for s in range(n)
                        ],
                        axis=0,
                    )
                tiles.append(tile)
            top = functools.reduce(
                jnp.maximum, [jnp.max(t, axis=0, keepdims=True) for t in tiles]
            )
            tiles = [jnp.exp2(t - top) for t in tiles]
            total = sum(jnp.sum(t, axis=0, keepdims=True) for t in tiles)
            inverse = 1.0 / total
            mixed = jnp.zeros((HEAD_DIM, columns), F32)
            for half, tile in enumerate(tiles):
                probs = tile * inverse
                if span == 0:
                    low_ref[group] = probs
                else:
                    high_ref[group, half * n * rows : (half + 1) * n * rows] = probs
                mixed += nn(vals_t[half], probs.astype(BF16))
            out = mixed.T.astype(BF16)
            for i in range(per_group):
                h = group * per_group + i
                att_ref[
                    span * rows : (span + 1) * rows, h * HEAD_DIM : (h + 1) * HEAD_DIM
                ] = out[i * rows : (i + 1) * rows]


def project_kernel(width, offsets, a_ref, w_ref, *outs):
    head = lax.axis_index("head")
    for s, out in zip(offsets, outs):
        start = pl.multiple_of((head ^ s) * width, width)
        out[...] = nn(a_ref[...], w_ref[:, pl.ds(start, width)]).astype(out.dtype)


def hold_kernel(w_ref, o_ref, sem):
    copy = pltpu.make_async_copy(w_ref, o_ref, sem)
    copy.start()
    copy.wait()


def prepare_kernel(lang_ref, table_ref, residual_ref, low_ref, high_ref, scale_ref, gap_ref):
    rows = low_ref.shape[0]
    kinds = table_ref.shape[0]
    chosen = lang_ref[...] == lax.broadcasted_iota(jnp.int32, (2 * rows, kinds), 1)
    scale_ref[...] = jnp.dot(
        chosen.astype(F32),
        table_ref[...],
        precision=lax.Precision.HIGHEST,
        preferred_element_type=F32,
    )
    for span, target in ((0, low_ref), (1, high_ref)):
        part = slice(span * rows, (span + 1) * rows)
        gap_ref[part] = residual_ref[part].astype(F32) - target[...].astype(F32)


def backward_kernel(n, nh, rows, kv_local, per_group, width, q_ref, low_ref, high_ref, w_ref, *refs):
    kv_refs, g_refs, outs = refs[:n], refs[n : n + nh], refs[n + nh :]
    dq_ref, dkv_refs = outs[0], outs[1:]
    head = lax.axis_index("head")
    columns = per_group * rows
    scale = HEAD_DIM**-0.5
    grad = None
    for s in range(nh):
        start = pl.multiple_of((head ^ s) * width, width)
        part = nt(g_refs[s][...], w_ref[:, pl.ds(start, width)])
        grad = part if grad is None else grad + part
    grad = grad.astype(BF16)
    for group in range(kv_local):
        keys = [stacked_keys(kv_refs, part, rows, group) for part in (0, 1)]
        vals = [stacked_keys(kv_refs, part, rows, group) for part in (2, 3)]
        keys_t = [k.astype(F32).T.astype(BF16) for k in keys]
        grad_k, grad_v = [None, None], [None, None]
        for span in (0, 1):
            query = stacked_heads(q_ref, span, rows, group, per_group)
            out = stacked_heads(grad, span, rows, group, per_group)
            probs = (
                [low_ref[group]]
                if span == 0
                else [high_ref[group, h * n * rows : (h + 1) * n * rows] for h in (0, 1)]
            )
            terms = [p * nt(vals[half], out) for half, p in enumerate(probs)]
            delta = sum(jnp.sum(t, axis=0, keepdims=True) for t in terms)
            grad_q = jnp.zeros((HEAD_DIM, columns), F32)
            for half, (prob, term) in enumerate(zip(probs, terms)):
                step = (term - prob * delta).astype(BF16)
                grad_q += nn(keys_t[half], step)
                dv, dk = nn(prob.astype(BF16), out), nn(step, query)
                grad_v[half] = dv if grad_v[half] is None else grad_v[half] + dv
                grad_k[half] = dk if grad_k[half] is None else grad_k[half] + dk
            grad_q = (grad_q * scale).T
            for i in range(per_group):
                h = group * per_group + i
                dq_ref[span * rows : (span + 1) * rows, h * HEAD_DIM : (h + 1) * HEAD_DIM] = (
                    grad_q[i * rows : (i + 1) * rows]
                )
        cols = slice(group * HEAD_DIM, (group + 1) * HEAD_DIM)
        for half in (0, 1):
            for s, ref in enumerate(dkv_refs):
                block = slice(s * rows, (s + 1) * rows)
                ref[half * rows : (half + 1) * rows, cols] = (grad_k[half][block] * scale).astype(
                    ref.dtype
                )
                ref[(2 + half) * rows : (3 + half) * rows, cols] = grad_v[half][block].astype(
                    ref.dtype
                )


def reduce_blocks(blocks, axis):
    blocks = dict(enumerate(blocks))
    for bit in bits_of(lax.axis_size(axis)):
        for s in sorted((s for s in blocks if s & bit), reverse=True):
            got = across(blocks.pop(s).astype(BF16), axis, bit)
            blocks[s ^ bit] = blocks[s ^ bit].astype(F32) + got.astype(F32)
    return blocks[0]


def on_device(queries, keys, values, residual, targets, lang_ids, lang_scale, out_weight):
    n, nh = lax.axis_size("ctx"), lax.axis_size("head")
    rows = queries.shape[1]
    kv_width, q_width = keys.shape[2], queries.shape[2]
    kv_local, q_local = kv_width // HEAD_DIM, q_width // HEAD_DIM
    per_group = q_local // kv_local
    width = residual.shape[2]
    columns = per_group * rows

    kv_own = jnp.concatenate([keys, values]).reshape(4 * rows, kv_width)
    kv = gather_blocks(kv_own, "ctx")
    upper_targets = across(targets[1], "ctx", n - 1)
    weight = pl.pallas_call(
        hold_kernel,
        out_shape=pltpu.VMEM(out_weight.shape, BF16),
        in_specs=[pl.BlockSpec(memory_space=pltpu.HBM)],
        out_specs=VMEM,
        scratch_shapes=[pltpu.SemaphoreType.DMA],
        compiler_params=pltpu.CompilerParams(vmem_limit_bytes=1 << 20),
        name="hold",
    )(out_weight)
    flat_q = queries.reshape(2 * rows, q_width)
    attended, low_probs, high_probs = call(
        functools.partial(attention_kernel, n, rows, kv_local, per_group),
        (
            pltpu.VMEM((2 * rows, q_width), BF16),
            pltpu.VMEM((kv_local, n * rows, columns), F32),
            pltpu.VMEM((kv_local, 2 * n * rows, columns), F32),
        ),
        (flat_q, *kv),
        [VMEM] * (1 + n),
        16,
        "attention",
        cost(12 * n * rows * columns * HEAD_DIM * kv_local, 1 << 21),
    )
    row_scales, gap = call(
        prepare_kernel,
        (pltpu.VMEM((2 * rows, width), F32), pltpu.VMEM((2 * rows, width), F32)),
        (
            lang_ids.reshape(2 * rows, 1),
            lang_scale,
            residual.reshape(2 * rows, width),
            targets[0],
            upper_targets,
        ),
        [VMEM] * 5,
        16,
        "prepare",
    )
    order = sorted(range(nh), key=lambda s: (s & 1 == 0, -s))
    parts = {}
    for offsets in (order[: nh // 4], order[nh // 4 :]):
        got = call(
            functools.partial(project_kernel, width, offsets),
            tuple(pltpu.VMEM((2 * rows, width), BF16 if s & 1 else F32) for s in offsets),
            (attended, weight),
            [VMEM] * 2,
            16,
            "project",
            cost(4 * rows * q_width * width * len(offsets), q_width * width * 2 * len(offsets)),
        )
        parts.update(zip(offsets, got))
    projected = reduce_blocks([parts[s] for s in range(nh)], "head")
    grad_proj = ((gap + projected * row_scales) * row_scales).astype(BF16)
    grads = gather_blocks(grad_proj, "head")
    outs = call(
        functools.partial(backward_kernel, n, nh, rows, kv_local, per_group, width),
        (
            jax.ShapeDtypeStruct((2 * rows, q_width), F32),
            pltpu.VMEM((4 * rows, kv_width), F32),
            *(pltpu.VMEM((4 * rows, kv_width), BF16) for _ in range(n - 1)),
        ),
        (flat_q, low_probs, high_probs, weight, *kv, *grads),
        [VMEM] * (4 + n + nh),
        20,
        "backward",
        cost(1 << 31, 1 << 24),
    )
    grad_kv = reduce_blocks(outs[1:], "ctx")
    return (
        outs[0].reshape(2, rows, q_width),
        grad_kv[: 2 * rows].reshape(2, rows, kv_width),
        grad_kv[2 * rows :].reshape(2, rows, kv_width),
    )


def solution(mesh):
    split = P(None, ("groups", "ctx"), "head")
    in_specs = (
        split,
        split,
        split,
        split,
        split,
        P(None, ("groups", "ctx")),
        P(None, "head"),
        P("head", None),
    )
    return jax.shard_map(
        on_device, mesh=mesh, in_specs=in_specs, out_specs=(split, split, split), check_vma=False
    )
```

```python
import functools
import math

import jax
import jax.numpy as jnp
from jax import lax
from jax.experimental import pallas as pl
from jax.experimental.pallas import tpu as pltpu
from jax.sharding import PartitionSpec as P

HEAD_DIM = 128
BIG_NEG = -1e30
LOG2E = 1.4426950408889634
F32 = jnp.float32
BF16 = jnp.bfloat16
VMEM = pl.BlockSpec(memory_space=pltpu.VMEM)
ANY = pl.BlockSpec(memory_space=pl.ANY)


def across(block, axis, bit):
    count = lax.axis_size(axis)
    return lax.ppermute(block, axis, [(i, i ^ bit) for i in range(count)])


def bits_of(count):
    return [1 << b for b in range(count.bit_length() - 1)]


def gather_blocks(own, axis, first):
    blocks = {0: own}
    for bit in reversed(bits_of(lax.axis_size(axis))):
        for s in sorted(blocks):
            if s:
                blocks[s], blocks[bit], first = lax.optimization_barrier(
                    (blocks[s], blocks[bit], first)
                )
            blocks[s ^ bit] = [across(b, axis, bit) for b in blocks[s]]
    return [[blocks[s][i] for s in range(len(blocks))] for i in range(len(own))], first


def nt(a, b):
    return lax.dot_general(a, b, (((1,), (1,)), ((), ())), preferred_element_type=F32)


def nn(a, b):
    return jnp.dot(a, b, preferred_element_type=F32)


def call(body, out, args, mib, name, after=(), flops=0):
    count, extra = len(args), len(after)

    def padded(*refs):
        body(*refs[:count], *refs[count + extra :])

    return pl.pallas_call(
        padded,
        out_shape=out,
        in_specs=[VMEM] * count + [ANY] * extra,
        out_specs=jax.tree.map(lambda _: VMEM, out),
        compiler_params=pltpu.CompilerParams(vmem_limit_bytes=mib << 20),
        cost_estimate=cost(flops, 0),
        name=name,
    )(*args, *after)


def cost(flops, moved):
    return pl.CostEstimate(flops=flops, bytes_accessed=moved, transcendentals=0)


def stacked_heads(ref, span, rows, group, per_group):
    pieces = [
        ref[span * rows : (span + 1) * rows, h * HEAD_DIM : (h + 1) * HEAD_DIM]
        for h in range(group * per_group, (group + 1) * per_group)
    ]
    return jnp.concatenate(pieces, axis=0)


def stacked_keys(refs, part, rows, group):
    cols = slice(group * HEAD_DIM, (group + 1) * HEAD_DIM)
    return jnp.concatenate([r[part * rows : (part + 1) * rows, cols] for r in refs], axis=0)


def diagonal_mask(owner_xor, device, rows, columns, upper):
    owner = device ^ owner_xor
    key = lax.broadcasted_iota(jnp.int32, (rows, columns), 0)
    query = lax.broadcasted_iota(jnp.int32, (rows, columns), 1) & (rows - 1)
    ahead = (device - owner if upper else owner - device) * rows
    return key + ahead <= query


def attention_kernel(n, rows, kv_local, per_group, q_ref, *refs):
    k_refs, v_refs, (att_ref, low_ref, high_ref) = refs[:n], refs[n : 2 * n], refs[2 * n :]
    device = lax.axis_index("ctx")
    columns = per_group * rows
    scale = HEAD_DIM**-0.5 * LOG2E
    masks = {
        (s, upper): diagonal_mask(s, device, rows, columns, upper)
        for s in range(n)
        for upper in (False, True)
    }
    for group in range(kv_local):
        keys = [stacked_keys(k_refs, part, rows, group) for part in (0, 1)]
        vals = [stacked_keys(v_refs, part, rows, group) for part in (0, 1)]
        vals_t = [v.astype(F32).T.astype(BF16) for v in vals]
        for span in (0, 1):
            query = stacked_heads(q_ref, span, rows, group, per_group)
            tiles = []
            for half in range(span + 1):
                tile = nt(keys[half], query) * scale
                if half == span:
                    tile = jnp.concatenate(
                        [
                            jnp.where(
                                masks[s, span == 1], tile[s * rows : (s + 1) * rows], BIG_NEG
                            )
                            for s in range(n)
                        ],
                        axis=0,
                    )
                tiles.append(tile)
            top = functools.reduce(
                jnp.maximum, [jnp.max(t, axis=0, keepdims=True) for t in tiles]
            )
            tiles = [jnp.exp2(t - top) for t in tiles]
            total = sum(jnp.sum(t, axis=0, keepdims=True) for t in tiles)
            inverse = 1.0 / total
            mixed = jnp.zeros((HEAD_DIM, columns), F32)
            for half, tile in enumerate(tiles):
                probs = tile * inverse
                if span == 0:
                    low_ref[group] = probs
                else:
                    high_ref[group, half * n * rows : (half + 1) * n * rows] = probs
                mixed += nn(vals_t[half], probs.astype(BF16))
            out = mixed.T.astype(BF16)
            for i in range(per_group):
                h = group * per_group + i
                att_ref[
                    span * rows : (span + 1) * rows, h * HEAD_DIM : (h + 1) * HEAD_DIM
                ] = out[i * rows : (i + 1) * rows]


def project_kernel(width, offsets, a_ref, w_ref, *outs):
    head = lax.axis_index("head")
    for s, out in zip(offsets, outs):
        start = pl.multiple_of((head ^ s) * width, width)
        out[...] = nn(a_ref[...], w_ref[:, pl.ds(start, width)]).astype(out.dtype)


def hold_kernel(w_ref, target_ref, w_out, upper_out, sems):
    copies = [
        pltpu.make_async_copy(target_ref.at[1], upper_out, sems.at[0]),
        pltpu.make_async_copy(w_ref, w_out, sems.at[1]),
    ]
    for copy in copies:
        copy.start()
    for copy in copies:
        copy.wait()


def prepare_kernel(lang_ref, table_ref, residual_ref, target_ref, upper_ref, scale_ref, gap_ref):
    rows = upper_ref.shape[0]
    kinds = table_ref.shape[0]
    for span, target in ((0, target_ref.at[0]), (1, upper_ref)):
        part = slice(span * rows, (span + 1) * rows)
        chosen = lang_ref[span : span + 1] == lax.broadcasted_iota(jnp.int32, (kinds, rows), 0)
        scale_ref[part] = lax.dot_general(
            chosen.astype(F32),
            table_ref[...],
            (((0,), (0,)), ((), ())),
            precision=lax.Precision.HIGHEST,
            preferred_element_type=F32,
        )
        gap_ref[part] = residual_ref[part].astype(F32) - target[...].astype(F32)


def sum_kernel(cut, *refs):
    addends, out = refs[:-1], refs[-1]
    out[...] = sum(a[:, cut].astype(F32) for a in addends).astype(out.dtype)


def gradient_kernel(cut, scale_ref, gap_ref, got_ref, *refs):
    addends, out = refs[:-1], refs[-1]
    scale = scale_ref[:, cut]
    projected = sum((a[:, cut].astype(F32) for a in addends), got_ref[...].astype(F32))
    out[...] = ((gap_ref[:, cut] + projected * scale) * scale).astype(BF16)


def weighted(width, places, g_refs, w_ref):
    head = lax.axis_index("head")
    total = None
    for (s, first, size), g_ref in zip(places, g_refs):
        start = pl.multiple_of((head ^ s) * width + first, size)
        part = nt(g_ref[...], w_ref[:, pl.ds(start, size)])
        total = part if total is None else total + part
    return total


def weighted_kernel(width, places, w_ref, *refs):
    g_refs, (*more, out) = refs[: len(places)], refs[len(places) :]
    total = weighted(width, places, g_refs, w_ref)
    out[...] = total + more[0][...] if more else total


def value_gradient_kernel(n, places, rows, kv_local, per_group, width, *refs):
    w_ref, low_ref, high_ref, more_ref, *refs = refs
    g_refs, (grad_ref, *out_refs) = refs[: len(places)], refs[len(places) :]
    grad = (more_ref[...] + weighted(width, places, g_refs, w_ref)).astype(BF16)
    grad_ref[...] = grad
    for group in range(kv_local):
        cols = slice(group * HEAD_DIM, (group + 1) * HEAD_DIM)
        low_out, high_out = [
            stacked_heads(grad, span, rows, group, per_group) for span in (0, 1)
        ]
        for half in (0, 1):
            part = slice(half * n * rows, (half + 1) * n * rows)
            total = nn(high_ref[group, part].astype(BF16), high_out)
            if half == 0:
                total += nn(low_ref[group].astype(BF16), low_out)
            for s, ref in enumerate(out_refs):
                ref[half * rows : (half + 1) * rows, cols] = total[
                    s * rows : (s + 1) * rows
                ].astype(ref.dtype)


def key_gradient_kernel(n, rows, kv_local, per_group, grad_ref, q_ref, low_ref, high_ref, *refs):
    k_refs, v_refs, (dq_ref, *out_refs) = refs[:n], refs[n : 2 * n], refs[2 * n :]
    columns = per_group * rows
    scale = HEAD_DIM**-0.5
    for group in range(kv_local):
        keys = [stacked_keys(k_refs, part, rows, group) for part in (0, 1)]
        vals = [stacked_keys(v_refs, part, rows, group) for part in (0, 1)]
        keys_t = [k.astype(F32).T.astype(BF16) for k in keys]
        grad_k = [None, None]
        for span in (0, 1):
            query = stacked_heads(q_ref, span, rows, group, per_group)
            out = stacked_heads(grad_ref, span, rows, group, per_group)
            probs = (
                [low_ref[group]]
                if span == 0
                else [high_ref[group, h * n * rows : (h + 1) * n * rows] for h in (0, 1)]
            )
            terms = [p * nt(vals[half], out) for half, p in enumerate(probs)]
            delta = sum(jnp.sum(t, axis=0, keepdims=True) for t in terms)
            grad_q = jnp.zeros((HEAD_DIM, columns), F32)
            for half, (prob, term) in enumerate(zip(probs, terms)):
                step = (term - prob * delta).astype(BF16)
                grad_q += nn(keys_t[half], step)
                dk = nn(step, query)
                grad_k[half] = dk if grad_k[half] is None else grad_k[half] + dk
            grad_q = (grad_q * scale).T
            for i in range(per_group):
                h = group * per_group + i
                dq_ref[span * rows : (span + 1) * rows, h * HEAD_DIM : (h + 1) * HEAD_DIM] = (
                    grad_q[i * rows : (i + 1) * rows]
                )
        cols = slice(group * HEAD_DIM, (group + 1) * HEAD_DIM)
        for half in (0, 1):
            for s, ref in enumerate(out_refs):
                ref[half * rows : (half + 1) * rows, cols] = (
                    grad_k[half][s * rows : (s + 1) * rows] * scale
                ).astype(ref.dtype)


def reduce_blocks(blocks, axis):
    blocks = dict(enumerate(blocks))
    for bit in bits_of(lax.axis_size(axis)):
        for s in sorted((s for s in blocks if s & bit), reverse=True):
            got = across(blocks.pop(s).astype(BF16), axis, bit)
            blocks[s ^ bit] = blocks[s ^ bit].astype(F32) + got.astype(F32)
    return blocks[0]


def on_device(queries, keys, values, residual, targets, lang_ids, lang_scale, out_weight):
    n, nh = lax.axis_size("ctx"), lax.axis_size("head")
    rows = queries.shape[1]
    kv_width, q_width = keys.shape[2], queries.shape[2]
    kv_local, q_local = kv_width // HEAD_DIM, q_width // HEAD_DIM
    per_group = q_local // kv_local
    width = residual.shape[2]
    columns = per_group * rows

    all_rows = 2 * rows
    f32_rows = pltpu.VMEM((all_rows, width), F32)
    flat_q = queries.reshape(all_rows, q_width)
    weight, upper_targets = pl.pallas_call(
        hold_kernel,
        out_shape=(pltpu.VMEM(out_weight.shape, BF16), pltpu.VMEM(targets.shape[1:], BF16)),
        in_specs=[ANY] * 2,
        out_specs=(VMEM, VMEM),
        scratch_shapes=[pltpu.SemaphoreType.DMA((2,))],
        compiler_params=pltpu.CompilerParams(vmem_limit_bytes=50 << 20),
        cost_estimate=cost(0, 4 * math.prod(out_weight.shape)),
        name="hold",
    )(out_weight, targets)
    upper_targets = across(upper_targets, "ctx", n - 1)
    (key_blocks, value_blocks), weight = gather_blocks(
        [keys.reshape(all_rows, kv_width), values.reshape(all_rows, kv_width)], "ctx", weight
    )
    attended, low_probs, high_probs = call(
        functools.partial(attention_kernel, n, rows, kv_local, per_group),
        (
            pltpu.VMEM((all_rows, q_width), BF16),
            pltpu.VMEM((kv_local, n * rows, columns), F32),
            pltpu.VMEM((kv_local, 2 * n * rows, columns), F32),
        ),
        (flat_q, *key_blocks, *value_blocks),
        16,
        "attention",
    )
    row_scales, gap = call(
        prepare_kernel,
        (f32_rows, f32_rows),
        (
            lang_ids,
            lang_scale,
            residual.reshape(all_rows, width),
            targets,
            upper_targets,
        ),
        4,
        "prepare",
        flops=3 << 29,
    )

    half = width // 2
    cuts = [slice(0, half), slice(half, width)]
    bits = bits_of(nh)
    top = bits[-1]
    share = {}

    def project(offsets, after=()):
        for s in offsets:
            block = call(
                functools.partial(project_kernel, width, [s]),
                pltpu.VMEM((all_rows, width), BF16 if s & (top - 1) & 1 else F32),
                (attended, weight),
                8,
                "project",
                after=after,
            )
            share[s] = [block]

    def total(addends, cut, after=()):
        out = pltpu.VMEM((all_rows, cut.stop - cut.start), BF16)
        return call(functools.partial(sum_kernel, cut), out, addends, 4, "sum", after=after)

    def reduce_to(base):
        for bit in bits[:-1]:
            for s in sorted((s for s in share if s & bit and s & top == base), reverse=True):
                addends = share.pop(s)
                whole = total(addends, slice(0, width)) if len(addends) > 1 else addends[0]
                share[s ^ bit].append(across(whole, "head", bit))

    upper_half = range(nh - 1, top - 1, -1)
    firsts = [s for s in upper_half if s & (top - 1) & 1]
    if firsts:
        project(firsts)
    project([s for s in upper_half if s not in firsts])
    reduce_to(top)
    addends = share.pop(top)
    sent = [total(addends, cut, (gap,)) for cut in cuts]
    got = [across(block, "head", top) for block in sent]
    project(range(top - 1, -1, -1), after=sent)
    reduce_to(0)
    blocks = {}
    for c, cut in enumerate(cuts):
        blocks[0, c] = call(
            functools.partial(gradient_kernel, cut),
            pltpu.VMEM((all_rows, half), BF16),
            (row_scales, gap, got[c], *share[0]),
            4,
            "gradient",
        )
        blocks[top, c] = across(blocks[0, c], "head", top)
    for bit in reversed(bits[:-1]):
        for s, c in sorted(blocks):
            blocks[s ^ bit, c] = across(blocks[s, c], "head", bit)
    near = [k for k in sorted(blocks) if k[0] < top]
    far = [(s, 0) for s in range(top, nh)] + [(s, 1) for s in range(top, nh)]
    grad = ()
    for used in (near, far[: top + 1]):
        places = [(s, c * half, half) for s, c in used]
        out = call(
            functools.partial(weighted_kernel, width, places),
            pltpu.VMEM((all_rows, q_width), F32),
            (weight, *(blocks[k] for k in used), *grad),
            8,
            "weighted",
            flops=1 << 31,
        )
        grad = (out,)
    last = far[top + 1 :]
    places = [(s, c * half, half) for s, c in last]
    shares = (
        pltpu.VMEM((all_rows, kv_width), F32),
        *(pltpu.VMEM((all_rows, kv_width), BF16) for _ in range(n - 1)),
    )
    grad_attended, *grad_values = call(
        functools.partial(
            value_gradient_kernel, n, places, rows, kv_local, per_group, width
        ),
        (pltpu.VMEM((all_rows, q_width), BF16), *shares),
        (weight, low_probs, high_probs, *grad, *(blocks[k] for k in last)),
        16,
        "value_gradient",
    )
    grad_queries, *grad_keys = call(
        functools.partial(key_gradient_kernel, n, rows, kv_local, per_group),
        (jax.ShapeDtypeStruct((all_rows, q_width), F32), *shares),
        (grad_attended, flat_q, low_probs, high_probs, *key_blocks, *value_blocks),
        16,
        "key_gradient",
        flops=1 << 31,
    )
    grad_values = reduce_blocks(grad_values, "ctx")
    grad_keys = reduce_blocks(grad_keys, "ctx")
    return (
        grad_queries.reshape(2, rows, q_width),
        grad_keys.reshape(2, rows, kv_width),
        grad_values.reshape(2, rows, kv_width),
    )


def solution(mesh):
    split = P(None, ("groups", "ctx"), "head")
    in_specs = (
        split,
        split,
        split,
        split,
        split,
        P(None, ("groups", "ctx")),
        P(None, "head"),
        P("head", None),
    )
    return jax.shard_map(
        on_device, mesh=mesh, in_specs=in_specs, out_specs=(split, split, split), check_vma=False
    )
```

```python
import functools
import math

import jax
import jax.numpy as jnp
from jax import lax
from jax.experimental import pallas as pl
from jax.experimental.pallas import tpu as pltpu
from jax.sharding import PartitionSpec as P

HEAD_DIM = 128
BIG_NEG = -1e30
LOG2E = 1.4426950408889634
F32 = jnp.float32
BF16 = jnp.bfloat16
PREPARE, SPREAD, KEYS, QUERIES, PROJECT, SECOND = 3 << 31, 1 << 31, 1 << 31, 1 << 31, 1 << 28, 1 << 30
VMEM = pl.BlockSpec(memory_space=pltpu.VMEM)
ANY = pl.BlockSpec(memory_space=pl.ANY)


def across(block, axis, bit):
    count = lax.axis_size(axis)
    return lax.ppermute(block, axis, [(i, i ^ bit) for i in range(count)])


def bits_of(count):
    return [1 << b for b in range(count.bit_length() - 1)]


def gather_blocks(own, axis, first):
    blocks = {0: own}
    for bit in reversed(bits_of(lax.axis_size(axis))):
        for s in sorted(blocks):
            if s:
                ahead, *others = blocks[s]
                ahead, first = lax.optimization_barrier((ahead, first))
                blocks[s] = [ahead, *others]
            blocks[s ^ bit] = [across(b, axis, bit) for b in blocks[s]]
    return [[blocks[s][i] for s in range(len(blocks))] for i in range(len(own))], first


def nt(a, b):
    return lax.dot_general(a, b, (((1,), (1,)), ((), ())), preferred_element_type=F32)


def nn(a, b):
    return jnp.dot(a, b, preferred_element_type=F32)


def call(body, out, args, mib, name, after=(), flops=0):
    count, extra = len(args), len(after)

    def padded(*refs):
        body(*refs[:count], *refs[count + extra :])

    return pl.pallas_call(
        padded,
        out_shape=out,
        in_specs=[VMEM] * count + [ANY] * extra,
        out_specs=jax.tree.map(lambda _: VMEM, out),
        compiler_params=pltpu.CompilerParams(vmem_limit_bytes=mib << 20),
        cost_estimate=cost(flops, 0),
        name=name,
    )(*args, *after)


def cost(flops, moved):
    return pl.CostEstimate(flops=flops, bytes_accessed=moved, transcendentals=0)


def stacked_heads(ref, span, rows, group, per_group):
    pieces = [
        ref[span * rows : (span + 1) * rows, h * HEAD_DIM : (h + 1) * HEAD_DIM]
        for h in range(group * per_group, (group + 1) * per_group)
    ]
    return jnp.concatenate(pieces, axis=0)


def stacked_keys(refs, part, rows, group):
    cols = slice(group * HEAD_DIM, (group + 1) * HEAD_DIM)
    return jnp.concatenate([r[part * rows : (part + 1) * rows, cols] for r in refs], axis=0)


def diagonal_mask(owner_xor, device, rows, columns, upper):
    owner = device ^ owner_xor
    key = lax.broadcasted_iota(jnp.int32, (rows, columns), 0)
    query = lax.broadcasted_iota(jnp.int32, (rows, columns), 1) & (rows - 1)
    ahead = (device - owner if upper else owner - device) * rows
    return key + ahead <= query


def attention_kernel(n, rows, kv_local, per_group, q_ref, *refs):
    k_refs, v_refs, (att_ref, low_ref, high_ref) = refs[:n], refs[n : 2 * n], refs[2 * n :]
    device = lax.axis_index("ctx")
    columns = per_group * rows
    scale = HEAD_DIM**-0.5 * LOG2E
    masks = {
        (s, upper): diagonal_mask(s, device, rows, columns, upper)
        for s in range(n)
        for upper in (False, True)
    }
    part = n * rows
    stores = (low_ref, high_ref)
    for group in range(kv_local):
        keys = [stacked_keys(k_refs, half, rows, group) for half in (0, 1)]
        for span in (0, 1):
            query = stacked_heads(q_ref, span, rows, group, per_group)
            for half in range(span + 1):
                tile = nt(keys[half], query) * scale
                for s in range(n):
                    block = tile[s * rows : (s + 1) * rows]
                    if half == span:
                        block = jnp.where(masks[s, span == 1], block, BIG_NEG)
                    first = half * part + s * rows
                    stores[span][group, first : first + rows] = block
    for group in range(kv_local):
        vals_t = [stacked_keys(v_refs, half, rows, group).T for half in (0, 1)]
        for span in (0, 1):
            store = stores[span]
            tiles = [store[group, h * part : (h + 1) * part] for h in range(span + 1)]
            top = functools.reduce(
                jnp.maximum, [jnp.max(t, axis=0, keepdims=True) for t in tiles]
            )
            tiles = [jnp.exp2(t - top) for t in tiles]
            inverse = 1.0 / sum(jnp.sum(t, axis=0, keepdims=True) for t in tiles)
            mixed = jnp.zeros((HEAD_DIM, columns), F32)
            for half, tile in enumerate(tiles):
                probs = tile * inverse
                store[group, half * part : (half + 1) * part] = probs
                mixed += nn(vals_t[half], probs.astype(BF16))
            out = mixed.astype(BF16).T
            for i in range(per_group):
                h = group * per_group + i
                att_ref[
                    span * rows : (span + 1) * rows, h * HEAD_DIM : (h + 1) * HEAD_DIM
                ] = out[i * rows : (i + 1) * rows]


def project_kernel(width, s, cut, a_ref, w_ref, out_ref):
    size = cut.stop - cut.start
    start = pl.multiple_of((lax.axis_index("head") ^ s) * width + cut.start, size)
    out_ref[...] = nn(a_ref[...], w_ref[:, pl.ds(start, size)]).astype(out_ref.dtype)


def hold_kernel(w_ref, target_ref, w_out, upper_out, sems):
    copies = [
        pltpu.make_async_copy(target_ref.at[1], upper_out, sems.at[0]),
        pltpu.make_async_copy(w_ref, w_out, sems.at[1]),
    ]
    for copy in copies:
        copy.start()
    for copy in copies:
        copy.wait()


def prepare_kernel(lang_ref, table_ref, residual_ref, target_ref, upper_ref, scale_ref, gap_ref):
    rows = upper_ref.shape[0]
    kinds = table_ref.shape[0]
    for span, target in ((0, target_ref.at[0]), (1, upper_ref)):
        part = slice(span * rows, (span + 1) * rows)
        chosen = lang_ref[span : span + 1] == lax.broadcasted_iota(jnp.int32, (kinds, rows), 0)
        scale_ref[part] = lax.dot_general(
            chosen.astype(F32),
            table_ref[...],
            (((0,), (0,)), ((), ())),
            precision=lax.Precision.HIGHEST,
            preferred_element_type=F32,
        )
        gap_ref[part] = residual_ref[part].astype(F32) - target[...].astype(F32)


def sum_kernel(*refs):
    addends, out = refs[:-1], refs[-1]
    out[...] = sum(a[...].astype(F32) for a in addends).astype(out.dtype)


def gradient_kernel(cut, scale_ref, gap_ref, got_ref, *refs):
    addends, out = refs[:-1], refs[-1]
    scale = scale_ref[:, cut]
    projected = sum((a[:, cut].astype(F32) for a in addends), got_ref[...].astype(F32))
    out[...] = ((gap_ref[:, cut] + projected * scale) * scale).astype(BF16)


def weighted(width, places, g_refs, w_ref):
    head = lax.axis_index("head")
    total = None
    for (s, first, size), g_ref in zip(places, g_refs):
        start = pl.multiple_of((head ^ s) * width + first, size)
        part = nt(g_ref[...], w_ref[:, pl.ds(start, size)])
        total = part if total is None else total + part
    return total


def weighted_kernel(width, places, w_ref, *refs):
    g_refs, (*more, out) = refs[: len(places)], refs[len(places) :]
    total = weighted(width, places, g_refs, w_ref)
    out[...] = total + more[0][...] if more else total


def value_gradient_kernel(n, places, rows, kv_local, per_group, width, *refs):
    w_ref, low_ref, high_ref, more_ref, *refs = refs
    g_refs, (grad_ref, *out_refs) = refs[: len(places)], refs[len(places) :]
    grad = (more_ref[...] + weighted(width, places, g_refs, w_ref)).astype(BF16)
    grad_ref[...] = grad
    for group in range(kv_local):
        cols = slice(group * HEAD_DIM, (group + 1) * HEAD_DIM)
        low_out, high_out = [
            stacked_heads(grad, span, rows, group, per_group) for span in (0, 1)
        ]
        for half in (0, 1):
            part = slice(half * n * rows, (half + 1) * n * rows)
            total = nn(high_ref[group, part].astype(BF16), high_out)
            if half == 0:
                total += nn(low_ref[group].astype(BF16), low_out)
            for s, ref in enumerate(out_refs):
                ref[half * rows : (half + 1) * rows, cols] = total[
                    s * rows : (s + 1) * rows
                ].astype(ref.dtype)


def key_gradient_kernel(n, rows, kv_local, per_group, grad_ref, q_ref, low_ref, high_ref, *refs):
    v_refs, (low_step_ref, high_step_ref, *out_refs) = refs[:n], refs[n:]
    part = n * rows
    for group in range(kv_local):
        vals = [stacked_keys(v_refs, half, rows, group) for half in (0, 1)]
        grad_k = [None, None]
        for span in (0, 1):
            query = stacked_heads(q_ref, span, rows, group, per_group)
            out = stacked_heads(grad_ref, span, rows, group, per_group)
            prob_ref, step_ref = (low_ref, low_step_ref) if span == 0 else (high_ref, high_step_ref)
            probs = [prob_ref[group, h * part : (h + 1) * part] for h in range(span + 1)]
            terms = [p * nt(vals[half], out) for half, p in enumerate(probs)]
            delta = sum(jnp.sum(t, axis=0, keepdims=True) for t in terms)
            for half, (prob, term) in enumerate(zip(probs, terms)):
                step = (term - prob * delta).astype(BF16)
                step_ref[group, half * part : (half + 1) * part] = step
                dk = nn(step, query)
                grad_k[half] = dk if grad_k[half] is None else grad_k[half] + dk
        cols = slice(group * HEAD_DIM, (group + 1) * HEAD_DIM)
        scale = HEAD_DIM**-0.5
        for half in (0, 1):
            for s, ref in enumerate(out_refs):
                ref[half * rows : (half + 1) * rows, cols] = (
                    grad_k[half][s * rows : (s + 1) * rows] * scale
                ).astype(ref.dtype)


def query_gradient_kernel(n, rows, kv_local, per_group, low_ref, high_ref, *refs):
    k_refs, dq_ref = refs[:n], refs[n]
    part = n * rows
    scale = HEAD_DIM**-0.5
    for group in range(kv_local):
        keys_t = [
            stacked_keys(k_refs, half, rows, group).astype(F32).T.astype(BF16) for half in (0, 1)
        ]
        for span, step_ref in ((0, low_ref), (1, high_ref)):
            grad_q = sum(
                nn(keys_t[half], step_ref[group, half * part : (half + 1) * part])
                for half in range(span + 1)
            )
            grad_q = (grad_q * scale).T
            for i in range(per_group):
                h = group * per_group + i
                dq_ref[span * rows : (span + 1) * rows, h * HEAD_DIM : (h + 1) * HEAD_DIM] = (
                    grad_q[i * rows : (i + 1) * rows]
                )


def reduce_blocks(blocks, axis):
    blocks = dict(enumerate(blocks))
    for bit in bits_of(lax.axis_size(axis)):
        for s in sorted((s for s in blocks if s & bit), reverse=True):
            sent = blocks.pop(s).astype(BF16)
            got = across(sent, axis, bit)
            blocks[s ^ bit] = blocks[s ^ bit].astype(F32) + got.astype(F32)
    return blocks[0], sent


def on_device(queries, keys, values, residual, targets, lang_ids, lang_scale, out_weight):
    n, nh = lax.axis_size("ctx"), lax.axis_size("head")
    rows = queries.shape[1]
    kv_width, q_width = keys.shape[2], queries.shape[2]
    kv_local, q_local = kv_width // HEAD_DIM, q_width // HEAD_DIM
    per_group = q_local // kv_local
    width = residual.shape[2]
    columns = per_group * rows

    all_rows = 2 * rows
    f32_rows = pltpu.VMEM((all_rows, width), F32)
    flat_q = queries.reshape(all_rows, q_width)
    weight, upper_targets = pl.pallas_call(
        hold_kernel,
        out_shape=(pltpu.VMEM(out_weight.shape, BF16), pltpu.VMEM(targets.shape[1:], BF16)),
        in_specs=[ANY] * 2,
        out_specs=(VMEM, VMEM),
        scratch_shapes=[pltpu.SemaphoreType.DMA((2,))],
        compiler_params=pltpu.CompilerParams(vmem_limit_bytes=50 << 20),
        cost_estimate=cost(0, 4 * math.prod(out_weight.shape)),
        name="hold",
    )(out_weight, targets)
    upper_targets = across(upper_targets, "ctx", n - 1)
    (key_blocks, value_blocks), weight = gather_blocks(
        [keys.reshape(all_rows, kv_width), values.reshape(all_rows, kv_width)], "ctx", weight
    )
    attended, low_probs, high_probs = call(
        functools.partial(attention_kernel, n, rows, kv_local, per_group),
        (
            pltpu.VMEM((all_rows, q_width), BF16),
            pltpu.VMEM((kv_local, n * rows, columns), F32),
            pltpu.VMEM((kv_local, 2 * n * rows, columns), F32),
        ),
        (flat_q, *key_blocks, *value_blocks),
        16,
        "attention",
    )
    half = width // 2
    cuts = [slice(0, half), slice(half, width)]
    bits = bits_of(nh)
    top = bits[-1]
    share = {}

    def project(offsets, ranges, after=()):
        for s in offsets:
            for c, cut in enumerate(ranges):
                block = call(
                    functools.partial(project_kernel, width, s, cut),
                    pltpu.VMEM(
                        (all_rows, cut.stop - cut.start), BF16 if s & (top - 1) & 1 else F32
                    ),
                    (attended, weight),
                    8,
                    "project",
                    after=after,
                    flops=PROJECT if after else (0 if s & 1 else SECOND),
                )
                share[s, c] = [block]

    def total(addends):
        if len(addends) == 1 and addends[0].dtype == BF16:
            return addends[0]
        return call(sum_kernel, pltpu.VMEM(addends[0].shape, BF16), addends, 4, "sum")

    def reduce_to(base):
        for bit in bits[:-1]:
            for s, c in sorted((k for k in share if k[0] & bit and k[0] & top == base), reverse=True):
                share[s ^ bit, c].append(across(total(share.pop((s, c))), "head", bit))

    upper_half = range(nh - 1, top - 1, -1)
    firsts = [s for s in upper_half if s & (top - 1) & 1]
    project(firsts, cuts)
    project([s for s in upper_half if s not in firsts], cuts)
    reduce_to(top)
    sent = [total(share.pop((top, c))) for c in (0, 1)]
    got = [across(block, "head", top) for block in sent]
    row_scales, gap = call(
        prepare_kernel,
        (f32_rows, f32_rows),
        (
            lang_ids,
            lang_scale,
            residual.reshape(all_rows, width),
            targets,
            upper_targets,
        ),
        4,
        "prepare",
        after=sent,
        flops=PREPARE,
    )
    project(range(top - 1, -1, -1), [slice(0, width)], after=sent)
    reduce_to(0)
    blocks = {}
    for c, cut in enumerate(cuts):
        blocks[0, c] = call(
            functools.partial(gradient_kernel, cut),
            pltpu.VMEM((all_rows, half), BF16),
            (row_scales, gap, got[c], *share[0, 0]),
            4,
            "gradient",
        )
        blocks[top, c] = across(blocks[0, c], "head", top)

    def pass_on(places):
        for bit in reversed(bits[:-1]):
            for s, c in [k for k in places if k in blocks]:
                if (s ^ bit, c) not in blocks:
                    blocks[s ^ bit, c] = across(blocks[s, c], "head", bit)

    def spread(used, *more):
        return call(
            functools.partial(weighted_kernel, width, [(s, c * half, half) for s, c in used]),
            pltpu.VMEM((all_rows, q_width), F32),
            (weight, *(blocks[k] for k in used), *more),
            8,
            "weighted",
            flops=SPREAD,
        )

    near = [(s, c) for c in (0, 1) for s in range(top)]
    far = [[(s, c) for s in range(top, nh)] for c in (0, 1)]
    pass_on(near)
    grad = spread([k for k in near if not k[0]])
    blocks[top, 0], grad = lax.optimization_barrier((blocks[top, 0], grad))
    pass_on(far[0])
    if top > 1:
        grad = spread([k for k in near if k[0]], grad)
    grad = spread(far[0], grad)
    blocks[top, 1], grad = lax.optimization_barrier((blocks[top, 1], grad))
    pass_on(far[1])
    if far[1][:-1]:
        grad = spread(far[1][:-1], grad)
    last = far[1][-1:]
    places = [(s, c * half, half) for s, c in last]
    shares = (
        pltpu.VMEM((all_rows, kv_width), F32),
        *(pltpu.VMEM((all_rows, kv_width), BF16) for _ in range(n - 1)),
    )
    grad_attended, *grad_values = call(
        functools.partial(
            value_gradient_kernel, n, places, rows, kv_local, per_group, width
        ),
        (pltpu.VMEM((all_rows, q_width), BF16), *shares),
        (weight, low_probs, high_probs, grad, *(blocks[k] for k in last)),
        16,
        "value_gradient",
    )
    low_step, high_step, *grad_keys = call(
        functools.partial(key_gradient_kernel, n, rows, kv_local, per_group),
        (
            pltpu.VMEM(low_probs.shape, BF16),
            pltpu.VMEM(high_probs.shape, BF16),
            *shares,
        ),
        (grad_attended, flat_q, low_probs, high_probs, *value_blocks),
        16,
        "key_gradient",
        flops=KEYS,
    )
    grad_values, _ = reduce_blocks(grad_values, "ctx")
    grad_keys, sent = reduce_blocks(grad_keys, "ctx")
    grad_queries = call(
        functools.partial(query_gradient_kernel, n, rows, kv_local, per_group),
        jax.ShapeDtypeStruct((all_rows, q_width), F32),
        (low_step, high_step, *key_blocks),
        16,
        "query_gradient",
        after=[sent],
        flops=QUERIES,
    )
    return (
        grad_queries.reshape(2, rows, q_width),
        grad_keys.reshape(2, rows, kv_width),
        grad_values.reshape(2, rows, kv_width),
    )


def solution(mesh):
    split = P(None, ("groups", "ctx"), "head")
    in_specs = (
        split,
        split,
        split,
        split,
        split,
        P(None, ("groups", "ctx")),
        P(None, "head"),
        P("head", None),
    )
    return jax.shard_map(
        on_device, mesh=mesh, in_specs=in_specs, out_specs=(split, split, split), check_vma=False
    )
```
